32 devices in a mesh: gx: 4 (over z), gy: 8 (over y, x, core).
Axes of the slice: x: 2, y: 2, z: 4, core: 2. Of those that a mesh axis runs over, the one named last changes fastest.
Arguments:
- features: bfloat16 [32768, 256], P(('gx', 'gy')), may hold values from -6 to 6
- self_weight_one: bfloat16 [256, 256], replicated, may hold values from -0.375 to 0.375
- neigh_weight_one: bfloat16 [256, 256], replicated, may hold values from -1.5 to 1.5
- self_weight_two: bfloat16 [256, 256], replicated, may hold values from -0.375 to 0.375
- neigh_weight_two: bfloat16 [256, 256], replicated, may hold values from -1.5 to 1.5
- degree: int32 [32768], P(('gx', 'gy')), may hold values from 128 to 383
- local_tiles: bfloat16 [1024, 128, 128], P(('gx', 'gy')), may hold values from 0 to 1, as said below
- local_coord: int32 [1024, 2], P(('gx', 'gy')), may hold values from 0 to 7, as said below
- local_count: int32 [32], P(('gx', 'gy')), may hold values from 1 to 32, as said below
- send_block: int32 [256], P(('gx', 'gy')), may hold values from 0 to 7
- boundary_tiles: bfloat16 [256, 128, 128], P(('gx', 'gy')), may hold values from 0 to 1, as said below
- boundary_row: int32 [256], P(('gx', 'gy')), may hold values from 0 to 7
- hub_rows: int32 [256], P(('gx', 'gy')), may hold values from 0 to 1023
- hub_tiles: bfloat16 [256, 128, 128], P(('gx', 'gy')), may hold values from 0 to 1, as said below
- hub_coord: int32 [256, 2], P(('gx', 'gy')), may hold values from 0 to 7, as said below
Outputs:
- node_out: bfloat16 [32768, 256], P(('gx', 'gy'))
The draws below stay inside these ranges and needn't reach their ends.
Inputs may be any that keep to these rules, and one draw needn't show every extreme that they name: `local_tiles`: entries are 0 or 1. `boundary_tiles`: entries are 0 or 1. `hub_tiles`: entries are 0 or 1. `local_coord`: both columns are row blocks of the same device. `local_count`: some device has all 32 slots live. `hub_coord`: column 0 is a row block below 8, column 1 a hub block below 2.
All inputs are finite; a program needn't handle non-finite values.
Results may differ from the reference program's by a relative error of at most 0.005.
Values may be sent and summed in bfloat16 or wider, within the bound.
A program may use at most 64 MiB of HBM per device.

```python
import jax
import jax.numpy as jnp
from jax import lax

FEAT = 256
TILE = 128
NODES_DEV = 1024
LOCAL_MAX = 32
HUB_TILE_DEV = 8
HUB_DEV = 8
BLOCKS_DEV = 8
NODES = 32768
HUBS = 256
HUB_BLOCKS = 2
N_GY = 8
DEVICES = 32


def sparse_tiles(key, count, density):
    picks = jax.random.bernoulli(key, density, (count, TILE, TILE))
    return picks.astype(jnp.float32)


def draw_local_tiles(key, part):
    return sparse_tiles(jax.random.fold_in(key, 11), DEVICES * LOCAL_MAX, 0.1).astype(jnp.bfloat16)


def draw_boundary_tiles(key, part):
    return sparse_tiles(jax.random.fold_in(key, 12), DEVICES * N_GY, 0.1).astype(jnp.bfloat16)


def draw_hub_tiles(key, part):
    return sparse_tiles(jax.random.fold_in(key, 13), DEVICES * HUB_TILE_DEV, 0.25).astype(jnp.bfloat16)


def draw_local_coord(key, part):
    key_shift, key_cols = jax.random.split(jax.random.fold_in(key, 21))
    shifts = jax.random.randint(key_shift, (DEVICES, 1), 0, BLOCKS_DEV, dtype=jnp.int32)
    rows = (jnp.arange(LOCAL_MAX, dtype=jnp.int32)[None, :] + shifts) % BLOCKS_DEV
    cols = jax.random.randint(key_cols, (DEVICES, LOCAL_MAX), 0, BLOCKS_DEV, dtype=jnp.int32)
    return jnp.stack([rows, cols], axis=-1).reshape(DEVICES * LOCAL_MAX, 2)


def draw_local_count(key, part):
    key_one, key_two, key_pick = jax.random.split(jax.random.fold_in(key, 31), 3)
    first = jax.random.randint(key_one, (DEVICES,), 1, LOCAL_MAX + 1, dtype=jnp.int32)
    second = jax.random.randint(key_two, (DEVICES,), 1, LOCAL_MAX + 1, dtype=jnp.int32)
    picked = jax.random.randint(key_pick, (), 0, DEVICES, dtype=jnp.int32)
    counts = jnp.minimum(first, second)
    return jnp.where(jnp.arange(DEVICES, dtype=jnp.int32) == picked, LOCAL_MAX, counts).astype(jnp.int32)


def draw_hub_coord(key, part):
    key_rows, key_cols = jax.random.split(jax.random.fold_in(key, 41))
    rows = jax.random.randint(key_rows, (DEVICES * HUB_TILE_DEV,), 0, BLOCKS_DEV, dtype=jnp.int32)
    cols = jax.random.randint(key_cols, (DEVICES * HUB_TILE_DEV,), 0, HUB_BLOCKS, dtype=jnp.int32)
    return jnp.stack([rows, cols], axis=-1)


def with_ends(entries, rng, least, top_value):
    extent = entries.shape
    index_at = [jax.random.randint(jax.random.fold_in(rng, axis), (), 0, extent[axis]) for axis in range(len(extent))]
    entries = entries.at[tuple(index_at)].set(least)
    longest = extent.index(max(extent))
    index_at[longest] = (index_at[longest] + 1) % extent[longest]
    return entries.at[tuple(index_at)].set(top_value)


def block_scale(key, extent, cuts, smallest, top_value):
    level, own = 1.0, jax.random.fold_in(key, 6)
    for axis_at, shards_of in cuts:
        draws = jnp.exp(jax.random.uniform(jax.random.fold_in(own, axis_at), (shards_of,), jnp.float32, smallest / len(cuts), top_value / len(cuts)))
        level = level * jnp.repeat(draws, extent[axis_at] // shards_of).reshape([-1 if axis == axis_at else 1 for axis in range(len(extent))])
    return level


def normal_values(own_key, extent, scale, reach, shards=(), kind=jnp.bfloat16):
    level = block_scale(own_key, extent, shards, -0.22, 0.18) if shards else 1.0
    entries = jax.random.normal(own_key, extent, jnp.float32) * scale * level
    return jnp.minimum(jnp.maximum(entries, -reach), reach).astype(kind)


def setup_inputs(seed: int = 0) -> dict:
    arg_keys = jax.random.split(jax.random.key(seed), 16)
    return {
        "features": normal_values(arg_keys[0], (NODES, FEAT), 1.0, 6.0, ((0, 32),)),
        "self_weight_one": normal_values(arg_keys[1], (FEAT, FEAT), FEAT ** -0.5, 0.375),
        "neigh_weight_one": normal_values(arg_keys[2], (FEAT, FEAT), (FEAT // 16) ** -0.5, 1.5),
        "self_weight_two": normal_values(arg_keys[3], (FEAT, FEAT), FEAT ** -0.5, 0.375),
        "neigh_weight_two": normal_values(arg_keys[4], (FEAT, FEAT), (FEAT // 16) ** -0.5, 1.5),
        "degree": with_ends(jax.random.randint(arg_keys[5], (NODES,), TILE, 3 * TILE), jax.random.fold_in(arg_keys[5], 1), TILE, (3 * TILE) - 1).astype(jnp.int32),
        "local_tiles": draw_local_tiles(jax.random.fold_in(arg_keys[15], 71), 0),
        "local_coord": draw_local_coord(jax.random.fold_in(arg_keys[15], 71), 0),
        "local_count": draw_local_count(jax.random.fold_in(arg_keys[15], 71), 0),
        "send_block": with_ends(jax.random.randint(arg_keys[9], (DEVICES * N_GY,), 0, BLOCKS_DEV), jax.random.fold_in(arg_keys[9], 1), 0, BLOCKS_DEV - 1).astype(jnp.int32),
        "boundary_tiles": draw_boundary_tiles(jax.random.fold_in(arg_keys[15], 71), 0),
        "boundary_row": with_ends(jax.random.randint(arg_keys[11], (DEVICES * N_GY,), 0, BLOCKS_DEV), jax.random.fold_in(arg_keys[11], 1), 0, BLOCKS_DEV - 1).astype(jnp.int32),
        "hub_rows": with_ends(jax.random.randint(arg_keys[12], (HUBS,), 0, NODES_DEV), jax.random.fold_in(arg_keys[12], 1), 0, NODES_DEV - 1).astype(jnp.int32),
        "hub_tiles": draw_hub_tiles(jax.random.fold_in(arg_keys[15], 71), 0),
        "hub_coord": draw_hub_coord(jax.random.fold_in(arg_keys[15], 71), 0),
    }


def tile_sum(tiles, rows, sources, weight, block_count):
    product = jnp.einsum('kij,kjf->kif', tiles.astype(jnp.float32), sources.astype(jnp.float32))
    onehot = (rows[None, :] == jnp.arange(block_count, dtype=jnp.int32)[:, None]).astype(jnp.float32) * weight[None, :]
    flat = product.reshape(product.shape[0], -1)
    return jnp.dot(onehot, flat, precision=lax.Precision.HIGHEST).reshape(block_count, TILE, FEAT)

def layer(nodes_in, self_weight, neigh_weight, degree, local_tiles, local_coord, local_count, send_block, boundary_tiles, boundary_row, hub_rows, hub_tiles, hub_coord):
    owners = jnp.arange(HUBS, dtype=jnp.int32) // HUB_DEV
    hub_feats = nodes_in[owners * NODES_DEV + hub_rows].reshape(HUBS // TILE, TILE, FEAT)
    node_blocks = nodes_in.reshape(DEVICES, BLOCKS_DEV, TILE, FEAT)
    local_all = local_tiles.reshape(DEVICES, LOCAL_MAX, TILE, TILE)
    coord_all = local_coord.reshape(DEVICES, LOCAL_MAX, 2)
    bound_all = boundary_tiles.reshape(DEVICES, N_GY, TILE, TILE)
    brow_all = boundary_row.reshape(DEVICES, N_GY)
    sends = send_block.reshape(DEVICES, N_GY)
    hubt_all = hub_tiles.reshape(DEVICES, HUB_TILE_DEV, TILE, TILE)
    hubc_all = hub_coord.reshape(DEVICES, HUB_TILE_DEV, 2)
    degree_all = degree.reshape(DEVICES, NODES_DEV)

    def one_device(device):
        row_gx = device // N_GY
        col_gy = device % N_GY
        own = node_blocks[device]
        coords = coord_all[device]
        live_mask = (jnp.arange(LOCAL_MAX, dtype=jnp.int32) < local_count[device]).astype(jnp.float32)
        totals = tile_sum(local_all[device], coords[:, 0], own[coords[:, 1]], live_mask, BLOCKS_DEV)
        peers = row_gx * N_GY + jnp.arange(N_GY, dtype=jnp.int32)
        chosen = sends[peers, col_gy]
        received = node_blocks[peers, chosen]
        totals = totals + tile_sum(bound_all[device], brow_all[device], received, jnp.ones((N_GY,), jnp.float32), BLOCKS_DEV)
        hub_coords = hubc_all[device]
        totals = totals + tile_sum(hubt_all[device], hub_coords[:, 0], hub_feats[hub_coords[:, 1]], jnp.ones((HUB_TILE_DEV,), jnp.float32), BLOCKS_DEV)
        neigh = (totals.reshape(NODES_DEV, FEAT) / degree_all[device][:, None].astype(jnp.float32)).astype(jnp.bfloat16)
        linear = jnp.dot(own.reshape(NODES_DEV, FEAT), self_weight, preferred_element_type=jnp.float32)
        return linear + jnp.dot(neigh, neigh_weight, preferred_element_type=jnp.float32)
    linear_all = lax.map(one_device, jnp.arange(DEVICES, dtype=jnp.int32))
    return linear_all.reshape(NODES, FEAT)

def reference(features, self_weight_one, neigh_weight_one, self_weight_two, neigh_weight_two, degree, local_tiles, local_coord, local_count, send_block, boundary_tiles, boundary_row, hub_rows, hub_tiles, hub_coord):
    graph = (degree, local_tiles, local_coord, local_count, send_block, boundary_tiles, boundary_row, hub_rows, hub_tiles, hub_coord)
    linear_one = layer(features, self_weight_one, neigh_weight_one, *graph)
    relu_one = jnp.maximum(linear_one, 0.0)
    scale = lax.rsqrt(lax.optimization_barrier(jnp.mean(relu_one * relu_one, axis=-1, keepdims=True)) + 1e-06)
    hidden = (relu_one * scale).astype(jnp.bfloat16)
    linear_two = layer(hidden, self_weight_two, neigh_weight_two, *graph)
    return linear_two.astype(jnp.bfloat16)
```

```python
import functools

import jax
import jax.numpy as jnp
from jax import lax
from jax.experimental import pallas as pl
from jax.experimental.pallas import tpu as pltpu
from jax.sharding import PartitionSpec as P

MESH = pl.DeviceIdType.MESH
GROUP = 8
LANES = 128
KEY_STEP = 64
F32 = jnp.float32
BF16 = jnp.bfloat16
I32 = jnp.int32


def kernel(
    n_gx,
    n_gy,
    dense_hubs,
    deg,
    lcoord,
    lcount,
    send,
    brow,
    hrows,
    hcoord,
    feat_any,
    ws1_any,
    wn1_any,
    ws2_any,
    wn2_any,
    ltiles_any,
    btiles_any,
    htiles_any,
    out_ref,
    feat,
    ws1,
    wn1,
    ws2,
    wn2,
    tiles,
    btiles,
    plan_vec,
    plan,
    prefix,
    near,
    hubm,
    boundm,
    hub_src,
    obuf,
    inc,
    hub,
    hub_all,
    hidden,
    acc,
    own_part,
    rdeg,
    wide,
    load_sem,
    plan_sem,
    block_send,
    block_recv,
    row_send,
    row_recv,
    col_send,
    col_recv,
):
    gx = lax.axis_index("gx")
    gy = lax.axis_index("gy")
    blocks, tile, width = feat.shape
    nodes = blocks * tile
    n_local = ltiles_any.shape[0]
    n_hub = htiles_any.shape[0]
    hub_blocks = hub_all.shape[0]
    bound_groups = n_gy // GROUP
    hub_dev = hrows.shape[0]
    local_cells = blocks * blocks
    n_cells = local_cells + (blocks * hub_blocks if dense_hubs else 0)
    n_sorted = n_local + (n_hub if dense_hubs else 0)

    def peer(k):
        place, other = 1, 0
        while place < n_gy:
            other += lax.rem(lax.div(gy, place) + lax.div(k, place), 2) * place
            place *= 2
        return other

    barrier = pltpu.get_barrier_semaphore()
    for k in range(1, n_gx):
        pl.semaphore_signal(
            barrier, inc=1, device_id=(lax.rem(gx + k, n_gx), gy), device_id_type=MESH
        )
    for k in reversed(range(1, n_gy)):
        pl.semaphore_signal(
            barrier, inc=1, device_id=(gx, peer(k)), device_id_type=MESH
        )

    loads = [
        pltpu.make_async_copy(src, dst, load_sem.at[i])
        for i, (src, dst) in enumerate(
            (
                (feat_any, feat),
                (ltiles_any, tiles.at[0:n_local]),
                (btiles_any, btiles),
                (htiles_any, tiles.at[n_local : n_local + n_hub]),
                (ws1_any, ws1),
                (wn1_any, wn1),
                (ws2_any, ws2),
                (wn2_any, wn2),
            )
        )
    ]
    for load in loads:
        load.start()

    def row_copy(layer, k):
        slot = hub.at[layer, gx, gy]
        return pltpu.make_async_remote_copy(
            src_ref=slot,
            dst_ref=slot,
            send_sem=row_send.at[layer, k],
            recv_sem=row_recv.at[layer, k],
            device_id=(gx, peer(k)),
            device_id_type=MESH,
        )

    def col_copy(layer, k):
        slot = hub.at[layer, gx]
        return pltpu.make_async_remote_copy(
            src_ref=slot,
            dst_ref=slot,
            send_sem=col_send.at[layer, k],
            recv_sem=col_recv.at[layer, k],
            device_id=(lax.rem(gx + k, n_gx), gy),
            device_id_type=MESH,
        )

    def block_copy(layer, k):
        return pltpu.make_async_remote_copy(
            src_ref=obuf.at[layer, k],
            dst_ref=inc.at[layer, k],
            send_sem=block_send.at[layer, k],
            recv_sem=block_recv.at[layer, k],
            device_id=(gx, peer(k)),
            device_id_type=MESH,
        )

    def pick_hubs(layer, src):
        wide[...] = src[...].reshape(nodes, width).astype(F32)
        row = lax.broadcasted_iota(I32, (hub_dev, width), 0)
        rows = jnp.zeros((hub_dev, width), F32)
        for k in range(hub_dev):
            value = jnp.broadcast_to(wide[pl.ds(hrows[k], 1), :], (hub_dev, width))
            rows = jnp.where(row == k, value, rows)
        hub[layer, gx, gy] = rows.astype(BF16)

    def fill_block(layer, src, k):
        obuf[layer, k] = src[send[peer(k)]]

    def start_rows(layer):
        for k in range(1, n_gy):
            row_copy(layer, k).start()

    def pass_rows_on(layer):
        for k in range(1, n_gy):
            row_copy(layer, k).wait_recv()
        for k in range(1, n_gx):
            col_copy(layer, k).start()

    def make_plan():
        count = lcount[0]
        lane = lax.broadcasted_iota(I32, (8, LANES), 1)
        sub = lax.broadcasted_iota(I32, (8, LANES), 0)
        far = jnp.full((8, LANES), LANES * KEY_STEP, I32)
        keys_row, columns = far, []
        for t in range(n_sorted):
            if t < n_local:
                cell = jnp.where(
                    t < count, lcoord[0, t] * blocks + lcoord[1, t], LANES - 1
                )
            else:
                h = t - n_local
                cell = local_cells + hcoord[0, h] * hub_blocks + hcoord[1, h]
            key = cell * KEY_STEP + t
            keys_row = jnp.where(lane == t, key, keys_row)
            if t % 8 == 0:
                columns.append(far)
            columns[-1] = jnp.where(sub == t % 8, key, columns[-1])
        order = jnp.zeros((8, LANES), I32)
        ends = jnp.zeros((8, LANES), I32)
        for i, column in enumerate(columns):
            less = jnp.where(keys_row < column, 1, 0)
            rank = jnp.sum(less, axis=1, keepdims=True)
            order += jnp.where(lane == rank, sub + 8 * i, 0)
            ends += jnp.where(lax.shift_right_logical(column, 6) <= lane, 1, 0)
        plan_vec[0] = jnp.broadcast_to(jnp.sum(order, axis=0, keepdims=True), (8, LANES))
        plan_vec[1] = jnp.broadcast_to(jnp.sum(ends, axis=0, keepdims=True), (8, LANES))

    plan_copy = pltpu.make_async_copy(plan_vec, plan, plan_sem)

    def build_near():
        def body(j, run):
            run = run + tiles[plan[0, 0, j]]
            prefix[j + 1] = run
            return run

        prefix[0] = jnp.zeros((tile, tile), BF16)
        lax.fori_loop(0, n_sorted, body, jnp.zeros((tile, tile), BF16), unroll=8)
        last = jnp.zeros((tile, tile), BF16)
        for cell in range(n_cells):
            now = prefix[plan[1, 0, cell]]
            if cell < local_cells:
                b, c = divmod(cell, blocks)
                near[b * tile : (b + 1) * tile, c * tile : (c + 1) * tile] = now - last
            else:
                b, c = divmod(cell - local_cells, hub_blocks)
                hubm[b * tile : (b + 1) * tile, c * tile : (c + 1) * tile] = now - last
            last = now

    def place(dst, u, values, row):
        for b in range(blocks):
            weight = jnp.where(row == b, 1.0, 0.0).astype(BF16)
            dst[b * tile : (b + 1) * tile, u * tile : (u + 1) * tile] = values * weight

    def place_bound():
        def body(g, carry):
            for u in range(GROUP):
                p = peer(g * GROUP + u)
                place(boundm.at[g], u, btiles[p], brow[p])
            return carry

        lax.fori_loop(0, bound_groups, body, 0)

    def place_hub():
        for u in range(n_hub):
            place(hubm, u, tiles[n_local + u], hcoord[0, u])

    def local_work(src, self_weight):
        whole = src[...].reshape(nodes, width)
        own_part[...] = jnp.dot(whole, self_weight[...], preferred_element_type=F32)
        acc[...] = jnp.dot(near[...], whole, preferred_element_type=F32)

    def bound_sum(layer, rows, start, stop):
        first = (bound_groups - 1) * GROUP
        return jnp.dot(
            boundm[bound_groups - 1, rows, start * tile : stop * tile],
            inc[layer, first + start : first + stop].reshape((stop - start) * tile, width),
            preferred_element_type=F32,
        )

    def wait_blocks(layer, start, stop):
        for k in range(max(start, 1), stop):
            block_copy(layer, k).wait_recv()

    def early_bound(layer):
        for g in range(bound_groups - 1):
            wait_blocks(layer, g * GROUP, (g + 1) * GROUP)
            acc[...] += jnp.dot(
                boundm[g],
                inc[layer, g * GROUP : (g + 1) * GROUP].reshape(GROUP * tile, width),
                preferred_element_type=F32,
            )
        wait_blocks(layer, n_gy - 8, n_gy - 2)
        acc[...] += bound_sum(layer, slice(0, nodes), 0, 6)

    def gather_hubs(layer):
        for k in range(1, n_gx):
            col_copy(layer, k).wait_recv()
        hub_all[...] = hub[layer].astype(F32).reshape(hub_all.shape).astype(BF16)
        for u in range(hub_src.shape[0]):
            hub_src[u] = hub_all[u] if dense_hubs else hub_all[hcoord[1, u]]

    def combine(layer, b, neigh_weight):
        rows = slice(2 * b * tile, 2 * (b + 1) * tile)
        inverse = rdeg[rows, :]
        total = (
            acc[rows, :]
            + jnp.dot(
                hubm[rows, :],
                hub_src[...].reshape(hub_src.shape[0] * tile, width),
                preferred_element_type=F32,
            )
            + bound_sum(layer, rows, 6, 8)
        )
        neigh = (total * jnp.concatenate([inverse, inverse], axis=1)).astype(BF16)
        return own_part[rows, :] + jnp.dot(
            neigh, neigh_weight[...], preferred_element_type=F32
        )

    loads[0].wait()
    pick_hubs(0, feat)
    for k in range(1, n_gy):
        fill_block(0, feat, k)
    pl.semaphore_wait(barrier, n_gy - 1 + n_gx - 1)
    start_rows(0)
    for k in range(1, n_gy):
        block_copy(0, k).start()
    make_plan()
    plan_copy.start()
    inc[0, 0] = feat[send[gy]]
    for b in range(blocks):
        inverse = 1.0 / deg[b : b + 1, :].astype(F32)
        rdeg[b * tile : (b + 1) * tile, :] = jnp.broadcast_to(inverse, (tile, tile)).T
    for load in loads[1:]:
        load.wait()
    place_bound()
    if not dense_hubs:
        place_hub()
    plan_copy.wait()
    build_near()
    pass_rows_on(0)
    local_work(feat, ws1)
    early_bound(0)
    gather_hubs(0)
    wait_blocks(0, n_gy - 2, n_gy)
    for b in range(blocks // 2):
        linear = jnp.maximum(combine(0, b, wn1), 0.0)
        scale = lax.rsqrt(jnp.mean(linear * linear, axis=-1, keepdims=True) + 1e-06)
        hidden[2 * b : 2 * b + 2] = (linear * scale).astype(BF16).reshape(2, tile, width)

    pick_hubs(1, hidden)
    start_rows(1)
    for k in range(1, n_gy):
        fill_block(1, hidden, k)
        block_copy(1, k).start()
    inc[1, 0] = hidden[send[gy]]
    local_work(hidden, ws2)
    pass_rows_on(1)
    early_bound(1)
    gather_hubs(1)
    wait_blocks(1, n_gy - 2, n_gy)
    for b in range(blocks // 2):
        out_ref[2 * b : 2 * b + 2] = combine(1, b, wn2).astype(BF16).reshape(2, tile, width)

    for layer in range(2):
        for k in range(1, n_gy):
            row_copy(layer, k).wait_send()
            block_copy(layer, k).wait_send()
        for k in range(1, n_gx):
            col_copy(layer, k).wait_send()


def store_kernel(src, dst, store_sem):
    stores = [
        pltpu.make_async_copy(src.at[b], dst.at[b], store_sem.at[b]) for b in range(src.shape[0])
    ]
    for store in stores:
        store.start()
    for store in stores:
        store.wait()


def per_device(
    n_gx,
    n_gy,
    features,
    self_weight_one,
    neigh_weight_one,
    self_weight_two,
    neigh_weight_two,
    degree,
    local_tiles,
    local_coord,
    local_count,
    send_block,
    boundary_tiles,
    boundary_row,
    hub_rows,
    hub_tiles,
    hub_coord,
):
    nodes, width = features.shape
    tile = local_tiles.shape[1]
    blocks = nodes // tile
    hub_dev = hub_rows.shape[0]
    n_local, n_hub = local_tiles.shape[0], hub_tiles.shape[0]
    hub_blocks = n_gx * n_gy * hub_dev // tile
    dense_hubs = blocks * (blocks + hub_blocks) < LANES and n_local + n_hub <= KEY_STEP
    hub_slots = hub_blocks if dense_hubs else n_hub
    vmem = pl.BlockSpec(memory_space=pltpu.VMEM)
    smem = pl.BlockSpec(memory_space=pltpu.SMEM)
    hbm = pl.BlockSpec(memory_space=pltpu.HBM)
    dma = pltpu.SemaphoreType.DMA
    out = pl.pallas_call(
        functools.partial(kernel, n_gx, n_gy, dense_hubs),
        out_shape=pltpu.VMEM((blocks, tile, width), BF16),
        in_specs=[vmem] + [smem] * 6 + [hbm] * 8,
        out_specs=vmem,
        scratch_shapes=[
            pltpu.VMEM((blocks, tile, width), BF16),
            pltpu.VMEM((width, width), BF16),
            pltpu.VMEM((width, width), BF16),
            pltpu.VMEM((width, width), BF16),
            pltpu.VMEM((width, width), BF16),
            pltpu.VMEM((n_local + n_hub, tile, tile), BF16),
            pltpu.VMEM(boundary_tiles.shape, BF16),
            pltpu.VMEM((2, 8, LANES), I32),
            pltpu.SMEM((2, 8, LANES), I32),
            pltpu.VMEM((n_local + n_hub + 1, tile, tile), BF16),
            pltpu.VMEM((nodes, nodes), BF16),
            pltpu.VMEM((nodes, hub_slots * tile), BF16),
            pltpu.VMEM((n_gy // GROUP, nodes, GROUP * tile), BF16),
            pltpu.VMEM((hub_slots, tile, width), BF16),
            pltpu.VMEM((2, n_gy, tile, width), BF16),
            pltpu.VMEM((2, n_gy, tile, width), BF16),
            pltpu.VMEM((2, n_gx, n_gy, hub_dev, width), BF16),
            pltpu.VMEM((hub_blocks, tile, width), BF16),
            pltpu.VMEM((blocks, tile, width), BF16),
            pltpu.VMEM((nodes, width), F32),
            pltpu.VMEM((nodes, width), F32),
            pltpu.VMEM((nodes, tile), F32),
            pltpu.VMEM((nodes, width), F32),
            dma((8,)),
            dma,
            dma((2, n_gy)),
            dma((2, n_gy)),
            dma((2, n_gy)),
            dma((2, n_gy)),
            dma((2, n_gx)),
            dma((2, n_gx)),
        ],
        compiler_params=pltpu.CompilerParams(
            collective_id=0, has_side_effects=True, vmem_limit_bytes=56 * 2**20
        ),
        name="sage_two_layers",
    )(
        degree.reshape(blocks, tile),
        local_coord.T,
        local_count,
        send_block,
        boundary_row,
        hub_rows,
        hub_coord.T,
        features.reshape(blocks, tile, width),
        self_weight_one,
        neigh_weight_one,
        self_weight_two,
        neigh_weight_two,
        local_tiles,
        boundary_tiles,
        hub_tiles,
    )
    out = pl.pallas_call(
        store_kernel,
        out_shape=jax.ShapeDtypeStruct((blocks, tile, width), BF16),
        in_specs=[vmem],
        out_specs=hbm,
        scratch_shapes=[dma((blocks,))],
        name="store_result",
    )(pltpu.with_memory_space_constraint(out, pltpu.VMEM))
    return out.reshape(nodes, width)


def solution(mesh):
    placed = (
        P(("gx", "gy"), None),
        P(),
        P(),
        P(),
        P(),
        P(("gx", "gy")),
        P(("gx", "gy"), None, None),
        P(("gx", "gy"), None),
        P(("gx", "gy")),
        P(("gx", "gy")),
        P(("gx", "gy"), None, None),
        P(("gx", "gy")),
        P(("gx", "gy")),
        P(("gx", "gy"), None, None),
        P(("gx", "gy"), None),
    )
    return jax.shard_map(
        functools.partial(per_device, mesh.shape["gx"], mesh.shape["gy"]),
        mesh=mesh,
        in_specs=placed,
        out_specs=P(("gx", "gy"), None),
        check_vma=False,
    )
```

```python
import functools

import jax
import jax.numpy as jnp
from jax import lax
from jax.experimental import pallas as pl
from jax.experimental.pallas import tpu as pltpu
from jax.sharding import PartitionSpec as P

MESH = pl.DeviceIdType.MESH
GROUP = 8
LANES = 128
KEY_STEP = 64
PIECES = 2
HALVES = 1
F32 = jnp.float32
BF16 = jnp.bfloat16
I32 = jnp.int32


def kernel(
    n_gx,
    n_gy,
    dense_hubs,
    deg_any,
    lcoord_any,
    lcount_any,
    send_any,
    brow_any,
    hrows_any,
    hcoord_any,
    feat_any,
    ws1_any,
    wn1_any,
    ws2_any,
    wn2_any,
    ltiles_any,
    btiles_any,
    htiles_any,
    out_ref,
    deg,
    lcoord,
    lcount,
    send,
    brow,
    hrows,
    hcoord,
    feat,
    ws1,
    wn1,
    ws2,
    wn2,
    tiles,
    btiles,
    plan_vec,
    plan,
    prefix,
    near,
    hubm,
    boundm,
    hub_src,
    obuf,
    inc,
    hub,
    hub_all,
    hidden,
    acc,
    own_part,
    rdeg,
    load_sem,
    plan_sem,
    above_in,
    block_send,
    block_recv,
    row_send,
    row_recv,
    col_send,
    col_recv,
):
    gx = lax.axis_index("gx")
    gy = lax.axis_index("gy")
    blocks, tile, width = feat.shape
    nodes = blocks * tile
    n_local = ltiles_any.shape[0]
    n_hub = htiles_any.shape[0]
    hub_blocks = hub_all.shape[0]
    bound_groups = n_gy // GROUP
    hub_dev = hrows.shape[0]
    piece = n_gy // PIECES
    part = blocks // 2
    half = tile // HALVES
    local_cells = blocks * blocks
    n_cells = local_cells + (blocks * hub_blocks if dense_hubs else 0)
    n_sorted = n_local + (n_hub if dense_hubs else 0)

    def peer(k):
        place, other = 1, 0
        while place < n_gy:
            other += lax.rem(lax.div(gy, place) + lax.div(k, place), 2) * place
            place *= 2
        return other

    barrier = pltpu.get_barrier_semaphore()
    for k in reversed(range(1, n_gy)):
        pl.semaphore_signal(
            barrier, inc=1, device_id=(gx, peer(k)), device_id_type=MESH
        )
    for k in range(1, n_gx):

        @pl.when(gx + k < n_gx)
        def greet_above():
            pl.semaphore_signal(
                barrier, inc=1, device_id=(gx + k, gy), device_id_type=MESH
            )

    def greet_below():
        for k in range(1, n_gx):

            @pl.when(gx >= k)
            def greet():
                pl.semaphore_signal(
                    above_in, inc=1, device_id=(gx - k, gy), device_id_type=MESH
                )

    loads = [
        pltpu.make_async_copy(src, dst, load_sem.at[i])
        for i, (src, dst) in enumerate(
            (
                (feat_any, feat),
                (ltiles_any, tiles.at[0:n_local]),
                (btiles_any, btiles),
                (htiles_any, tiles.at[n_local : n_local + n_hub]),
                (ws1_any, ws1),
                (wn1_any, wn1),
                (ws2_any, ws2),
                (wn2_any, wn2),
            )
        )
    ]
    small = [
        pltpu.make_async_copy(src, dst, load_sem.at[len(loads) + i])
        for i, (src, dst) in enumerate(
            (
                (send_any, send),
                (hrows_any, hrows),
                (deg_any, deg),
                (lcoord_any, lcoord),
                (lcount_any, lcount),
                (brow_any, brow),
                (hcoord_any, hcoord),
            )
        )
    ]
    loads[0].start()
    for load in small:
        load.start()
    for load in loads[1:]:
        load.start()

    def row_copy(layer, k):
        slot = hub.at[layer, gx, gy]
        return pltpu.make_async_remote_copy(
            src_ref=slot,
            dst_ref=slot,
            send_sem=row_send.at[layer, k],
            recv_sem=row_recv.at[layer, k],
            device_id=(gx, peer(k)),
            device_id_type=MESH,
        )

    def col_copy(layer, k, m):
        start = peer(m * piece) - lax.rem(gy, piece)
        slots = hub.at[layer, gx, pl.ds(start, piece)]
        return pltpu.make_async_remote_copy(
            src_ref=slots,
            dst_ref=slots,
            send_sem=col_send.at[layer, k, m],
            recv_sem=col_recv.at[layer, k, m],
            device_id=(lax.rem(gx + k, n_gx), gy),
            device_id_type=MESH,
        )

    def block_copy(layer, k, h):
        rows = pl.ds(h * half, half) if layer else pl.ds(0, tile)
        return pltpu.make_async_remote_copy(
            src_ref=obuf.at[layer, k, rows],
            dst_ref=inc.at[layer, k, rows],
            send_sem=block_send.at[layer, h, k],
            recv_sem=block_recv.at[layer, h, k],
            device_id=(gx, peer(k)),
            device_id_type=MESH,
        )

    def parts(layer):
        return range(HALVES if layer else 1)

    def chunk(s, h):
        return slice(s * part, (s + 1) * part), slice(h * half, (h + 1) * half)

    def pick(src, s, h):
        row = lax.broadcasted_iota(I32, (16, part * half), 0)
        lane = lax.broadcasted_iota(I32, (16, part * half), 1)
        wanted = jnp.full((16, part * half), -1, I32)
        for k in range(hub_dev):
            wanted = jnp.where(row == k, hrows[k], wanted)
        node = (s * part + lane // half) * tile + h * half + lane % half
        onehot = jnp.where(node == wanted, 1.0, 0.0).astype(BF16)
        return jnp.dot(onehot, src, preferred_element_type=F32)

    def start_rows(layer, picked):
        hub[layer, gx, gy] = picked[0:hub_dev].astype(BF16)
        for k in range(1, n_gy):
            row_copy(layer, k).start()

    def pass_rows_on(layer, m):
        for k in range(max(m * piece, 1), (m + 1) * piece):
            row_copy(layer, k).wait_recv()
        for k in range(1, n_gx):
            col_copy(layer, k, m).start()

    def make_plan():
        count = lcount[0]
        lane = lax.broadcasted_iota(I32, (8, LANES), 1)
        sub = lax.broadcasted_iota(I32, (8, LANES), 0)
        far = jnp.full((8, LANES), LANES * KEY_STEP, I32)
        keys_row, columns = far, []
        for t in range(n_sorted):
            if t < n_local:
                cell = jnp.where(
                    t < count, lcoord[0, t] * blocks + lcoord[1, t], LANES - 1
                )
            else:
                h = t - n_local
                cell = local_cells + hcoord[0, h] * hub_blocks + hcoord[1, h]
            key = cell * KEY_STEP + t
            keys_row = jnp.where(lane == t, key, keys_row)
            if t % 8 == 0:
                columns.append(far)
            columns[-1] = jnp.where(sub == t % 8, key, columns[-1])
        order = jnp.zeros((8, LANES), I32)
        ends = jnp.zeros((8, LANES), I32)
        for i, column in enumerate(columns):
            less = jnp.where(keys_row < column, 1, 0)
            rank = jnp.sum(less, axis=1, keepdims=True)
            order += jnp.where(lane == rank, sub + 8 * i, 0)
            ends += jnp.where(lax.shift_right_logical(column, 6) <= lane, 1, 0)
        plan_vec[0] = jnp.broadcast_to(jnp.sum(order, axis=0, keepdims=True), (8, LANES))
        plan_vec[1] = jnp.broadcast_to(jnp.sum(ends, axis=0, keepdims=True), (8, LANES))

    plan_copy = pltpu.make_async_copy(plan_vec, plan, plan_sem)

    def build_near():
        def body(j, run):
            run = run + tiles[plan[0, 0, j]]
            prefix[j + 1] = run
            return run

        prefix[0] = jnp.zeros((tile, tile), BF16)
        lax.fori_loop(0, n_sorted, body, jnp.zeros((tile, tile), BF16), unroll=8)
        last = jnp.zeros((tile, tile), BF16)
        for cell in range(n_cells):
            now = prefix[plan[1, 0, cell]]
            if cell < local_cells:
                b, c = divmod(cell, blocks)
                near[b, :, c * tile : (c + 1) * tile] = now - last
            else:
                b, c = divmod(cell - local_cells, hub_blocks)
                hubm[b, :, c * tile : (c + 1) * tile] = now - last
            last = now

    def place(dst, u, values, row):
        for b in range(blocks):
            weight = jnp.where(row == b, 1.0, 0.0).astype(BF16)
            dst[b, :, u * tile : (u + 1) * tile] = values * weight

    def place_bound():
        def body(g, carry):
            for u in range(GROUP):
                p = peer(g * GROUP + u)
                place(boundm.at[g], u, btiles[p], brow[p])
            return carry

        lax.fori_loop(0, bound_groups, body, 0)

    def place_hub():
        for u in range(n_hub):
            place(hubm, u, tiles[n_local + u], hcoord[0, u])

    def flat(values):
        return values.reshape(values.shape[0] * values.shape[1], values.shape[2])

    def own_work(src, self_weight):
        own_part[...] = jnp.dot(
            flat(src[...]), self_weight[...], preferred_element_type=F32
        ).reshape(own_part.shape)

    def local_work(src):
        acc[...] = jnp.dot(
            flat(near[...]), flat(src[...]), preferred_element_type=F32
        ).reshape(acc.shape)

    def wait_blocks(layer, start, stop):
        for k in range(max(start, 1), stop):
            for h in parts(layer):
                block_copy(layer, k, h).wait_recv()

    def bound_sum(layer, g, where, start, stop):
        sources = inc[layer, g * GROUP + start : g * GROUP + stop]
        return jnp.dot(
            flat(boundm[g, where[0], where[1], start * tile : stop * tile]),
            flat(sources),
            preferred_element_type=F32,
        )

    every = (slice(0, blocks), slice(0, tile))

    def early_bound(layer):
        for g in range(bound_groups):
            stop = GROUP if g < bound_groups - 1 else GROUP - 2
            wait_blocks(layer, g * GROUP, g * GROUP + stop)
            acc[...] += bound_sum(layer, g, every, 0, stop).reshape(acc.shape)

    def hub_work(layer):
        for m in range(PIECES):
            for k in range(1, n_gx):
                col_copy(layer, k, m).wait_recv()
        hub_all[...] = hub[layer].astype(F32).reshape(hub_all.shape).astype(BF16)
        for u in range(hub_src.shape[0]):
            hub_src[u] = hub_all[u] if dense_hubs else hub_all[hcoord[1, u]]
        acc[...] += jnp.dot(
            flat(hubm[...]), flat(hub_src[...]), preferred_element_type=F32
        ).reshape(acc.shape)

    def combine(layer, s, h, neigh_weight):
        where = chunk(s, h)
        inverse = flat(rdeg[where])
        total = flat(acc[where]) + bound_sum(layer, bound_groups - 1, where, 6, 8)
        neigh = (total * jnp.concatenate([inverse, inverse], axis=1)).astype(BF16)
        return flat(own_part[where]) + jnp.dot(
            neigh, neigh_weight[...], preferred_element_type=F32
        )

    small[0].wait()
    small[1].wait()
    loads[0].wait()
    picked = jnp.zeros((16, width), F32)
    for s in range(2):
        for h in range(HALVES):
            picked += pick(flat(feat[chunk(s, h)]), s, h)
    for k in range(1, n_gy):
        obuf[0, k] = feat[send[peer(k)]]
    pl.semaphore_wait(barrier, n_gy - 1 + gx)
    start_rows(0, picked)
    greet_below()
    for k in range(1, n_gy):
        block_copy(0, k, 0).start()
    for load in small[2:]:
        load.wait()
    make_plan()
    plan_copy.start()
    inc[0, 0] = feat[send[gy]]
    for b in range(blocks):
        inverse = 1.0 / deg[b : b + 1, :].astype(F32)
        rdeg[b] = jnp.broadcast_to(inverse, (tile, tile)).T
    for load in loads[1:]:
        load.wait()
    place_bound()
    if not dense_hubs:
        place_hub()
    plan_copy.wait()
    build_near()

    @pl.when(gx + 1 < n_gx)
    def wait_above():
        pl.semaphore_wait(above_in, n_gx - 1 - gx)

    for m in range(PIECES):
        pass_rows_on(0, m)
    own_work(feat, ws1)
    local_work(feat)
    early_bound(0)
    hub_work(0)
    wait_blocks(0, n_gy - 2, n_gy)
    picked = jnp.zeros((16, width), F32)
    for h in range(HALVES):
        for s in range(2):
            linear = jnp.maximum(combine(0, s, h, wn1), 0.0)
            scale = lax.rsqrt(jnp.mean(linear * linear, axis=-1, keepdims=True) + 1e-06)
            normed = (linear * scale).astype(BF16)
            hidden[chunk(s, h)] = normed.reshape(part, half, width)
            picked += pick(normed, s, h)
    start_rows(1, picked)
    for k in range(1, n_gy):
        obuf[1, k] = hidden[send[peer(k)]]
        block_copy(1, k, 0).start()
    inc[1, 0] = hidden[send[gy]]
    own_work(hidden, ws2)
    for m in range(PIECES):
        pass_rows_on(1, m)
    local_work(hidden)
    early_bound(1)
    hub_work(1)
    wait_blocks(1, n_gy - 2, n_gy)
    for h in range(HALVES):
        for s in range(2):
            out_ref[chunk(s, h)] = combine(1, s, h, wn2).astype(BF16).reshape(part, half, width)

    for layer in range(2):
        for k in range(1, n_gy):
            row_copy(layer, k).wait_send()
            for h in parts(layer):
                block_copy(layer, k, h).wait_send()
        for k in range(1, n_gx):
            for m in range(PIECES):
                col_copy(layer, k, m).wait_send()


def store_kernel(src, dst, store_sem):
    stores = [
        pltpu.make_async_copy(src.at[b], dst.at[b], store_sem.at[b]) for b in range(src.shape[0])
    ]
    for store in stores:
        store.start()
    for store in stores:
        store.wait()


def per_device(
    n_gx,
    n_gy,
    features,
    self_weight_one,
    neigh_weight_one,
    self_weight_two,
    neigh_weight_two,
    degree,
    local_tiles,
    local_coord,
    local_count,
    send_block,
    boundary_tiles,
    boundary_row,
    hub_rows,
    hub_tiles,
    hub_coord,
):
    nodes, width = features.shape
    tile = local_tiles.shape[1]
    blocks = nodes // tile
    hub_dev = hub_rows.shape[0]
    n_local, n_hub = local_tiles.shape[0], hub_tiles.shape[0]
    hub_blocks = n_gx * n_gy * hub_dev // tile
    dense_hubs = blocks * (blocks + hub_blocks) < LANES and n_local + n_hub <= KEY_STEP
    hub_slots = hub_blocks if dense_hubs else n_hub
    vmem = pl.BlockSpec(memory_space=pltpu.VMEM)
    hbm = pl.BlockSpec(memory_space=pltpu.HBM)
    dma = pltpu.SemaphoreType.DMA
    out = pl.pallas_call(
        functools.partial(kernel, n_gx, n_gy, dense_hubs),
        out_shape=pltpu.VMEM((blocks, tile, width), BF16),
        in_specs=[hbm] * 15,
        out_specs=vmem,
        scratch_shapes=[
            pltpu.VMEM((blocks, tile), I32),
            pltpu.SMEM((2, n_local), I32),
            pltpu.SMEM(local_count.shape, I32),
            pltpu.SMEM(send_block.shape, I32),
            pltpu.SMEM(boundary_row.shape, I32),
            pltpu.SMEM(hub_rows.shape, I32),
            pltpu.SMEM((2, n_hub), I32),
            pltpu.VMEM((blocks, tile, width), BF16),
            pltpu.VMEM((width, width), BF16),
            pltpu.VMEM((width, width), BF16),
            pltpu.VMEM((width, width), BF16),
            pltpu.VMEM((width, width), BF16),
            pltpu.VMEM((n_local + n_hub, tile, tile), BF16),
            pltpu.VMEM(boundary_tiles.shape, BF16),
            pltpu.VMEM((2, 8, LANES), I32),
            pltpu.SMEM((2, 8, LANES), I32),
            pltpu.VMEM((n_local + n_hub + 1, tile, tile), BF16),
            pltpu.VMEM((blocks, tile, nodes), BF16),
            pltpu.VMEM((blocks, tile, hub_slots * tile), BF16),
            pltpu.VMEM((n_gy // GROUP, blocks, tile, GROUP * tile), BF16),
            pltpu.VMEM((hub_slots, tile, width), BF16),
            pltpu.VMEM((2, n_gy, tile, width), BF16),
            pltpu.VMEM((2, n_gy, tile, width), BF16),
            pltpu.VMEM((2, n_gx, n_gy, hub_dev, width), BF16),
            pltpu.VMEM((hub_blocks, tile, width), BF16),
            pltpu.VMEM((blocks, tile, width), BF16),
            pltpu.VMEM((blocks, tile, width), F32),
            pltpu.VMEM((blocks, tile, width), F32),
            pltpu.VMEM((blocks, tile, tile), F32),
            dma((15,)),
            dma,
            pltpu.SemaphoreType.REGULAR,
            dma((2, HALVES, n_gy)),
            dma((2, HALVES, n_gy)),
            dma((2, n_gy)),
            dma((2, n_gy)),
            dma((2, n_gx, PIECES)),
            dma((2, n_gx, PIECES)),
        ],
        compiler_params=pltpu.CompilerParams(
            collective_id=0, has_side_effects=True, vmem_limit_bytes=56 * 2**20
        ),
        name="sage_two_layers",
    )(
        degree.reshape(blocks, tile),
        local_coord.T,
        local_count,
        send_block,
        boundary_row,
        hub_rows,
        hub_coord.T,
        features.reshape(blocks, tile, width),
        self_weight_one,
        neigh_weight_one,
        self_weight_two,
        neigh_weight_two,
        local_tiles,
        boundary_tiles,
        hub_tiles,
    )
    out = pl.pallas_call(
        store_kernel,
        out_shape=jax.ShapeDtypeStruct((blocks, tile, width), BF16),
        in_specs=[vmem],
        out_specs=hbm,
        scratch_shapes=[dma((blocks,))],
        name="store_result",
    )(pltpu.with_memory_space_constraint(out, pltpu.VMEM))
    return out.reshape(nodes, width)


def solution(mesh):
    placed = (
        P(("gx", "gy"), None),
        P(),
        P(),
        P(),
        P(),
        P(("gx", "gy")),
        P(("gx", "gy"), None, None),
        P(("gx", "gy"), None),
        P(("gx", "gy")),
        P(("gx", "gy")),
        P(("gx", "gy"), None, None),
        P(("gx", "gy")),
        P(("gx", "gy")),
        P(("gx", "gy"), None, None),
        P(("gx", "gy"), None),
    )
    return jax.shard_map(
        functools.partial(per_device, mesh.shape["gx"], mesh.shape["gy"]),
        mesh=mesh,
        in_specs=placed,
        out_specs=P(("gx", "gy"), None),
        check_vma=False,
    )
```

```python
import functools

import jax
import jax.numpy as jnp
from jax import lax
from jax.experimental import pallas as pl
from jax.experimental.pallas import tpu as pltpu
from jax.sharding import PartitionSpec as P

MESH = pl.DeviceIdType.MESH
GROUP = 8
LANES = 128
KEY_STEP = 64
PIECES = 2
HALVES = 1
F32 = jnp.float32
BF16 = jnp.bfloat16
I32 = jnp.int32


def kernel(
    n_gx,
    n_gy,
    dense_hubs,
    deg_any,
    lcoord_any,
    lcount_any,
    send_any,
    brow_any,
    hrows_any,
    hcoord_any,
    feat_any,
    ws1_any,
    wn1_any,
    ws2_any,
    wn2_any,
    ltiles_any,
    btiles_any,
    htiles_any,
    out_ref,
    deg,
    lcoord,
    lcount,
    send,
    brow,
    hrows,
    hcoord,
    feat,
    ws1,
    wn1,
    ws2,
    wn2,
    tiles,
    btiles,
    plan_vec,
    plan,
    prefix,
    near,
    hubm,
    boundm,
    hub_src,
    obuf,
    inc,
    hub,
    hub_all,
    hidden,
    acc,
    own_part,
    rdeg,
    hub_bound,
    load_sem,
    plan_sem,
    above_in,
    block_send,
    block_recv,
    row_send,
    row_recv,
    col_send,
    col_recv,
):
    gx = lax.axis_index("gx")
    gy = lax.axis_index("gy")
    blocks, tile, width = feat.shape
    nodes = blocks * tile
    n_local = ltiles_any.shape[0]
    n_hub = htiles_any.shape[0]
    hub_blocks = hub_all.shape[0]
    bound_groups = n_gy // GROUP
    hub_dev = hrows.shape[0]
    piece = n_gy // PIECES
    part = blocks // 2
    half = tile // HALVES
    local_cells = blocks * blocks
    n_cells = local_cells + (blocks * hub_blocks if dense_hubs else 0)
    n_sorted = n_local + (n_hub if dense_hubs else 0)

    def peer(k):
        place, other = 1, 0
        while place < n_gy:
            other += lax.rem(lax.div(gy, place) + lax.div(k, place), 2) * place
            place *= 2
        return other

    barrier = pltpu.get_barrier_semaphore()
    for k in reversed(range(1, n_gy)):
        pl.semaphore_signal(
            barrier, inc=1, device_id=(gx, peer(k)), device_id_type=MESH
        )
    for k in range(1, n_gx):

        @pl.when(gx + k < n_gx)
        def greet_above():
            pl.semaphore_signal(
                barrier, inc=1, device_id=(gx + k, gy), device_id_type=MESH
            )

    def greet_below():
        for k in range(1, n_gx):

            @pl.when(gx >= k)
            def greet():
                pl.semaphore_signal(
                    above_in, inc=1, device_id=(gx - k, gy), device_id_type=MESH
                )

    loads = [
        pltpu.make_async_copy(src, dst, load_sem.at[i])
        for i, (src, dst) in enumerate(
            (
                (feat_any, feat),
                (ltiles_any, tiles.at[0:n_local]),
                (btiles_any, btiles),
                (htiles_any, tiles.at[n_local : n_local + n_hub]),
                (ws1_any, ws1),
                (wn1_any, wn1),
                (ws2_any, ws2),
                (wn2_any, wn2),
            )
        )
    ]
    small = [
        pltpu.make_async_copy(src, dst, load_sem.at[len(loads) + i])
        for i, (src, dst) in enumerate(
            (
                (send_any, send),
                (hrows_any, hrows),
                (deg_any, deg),
                (lcoord_any, lcoord),
                (lcount_any, lcount),
                (brow_any, brow),
                (hcoord_any, hcoord),
            )
        )
    ]
    loads[0].start()
    for load in small:
        load.start()

    def row_copy(layer, k):
        slot = hub.at[layer, gx, gy]
        return pltpu.make_async_remote_copy(
            src_ref=slot,
            dst_ref=slot,
            send_sem=row_send.at[layer, k],
            recv_sem=row_recv.at[layer, k],
            device_id=(gx, peer(k)),
            device_id_type=MESH,
        )

    def col_copy(layer, k, m):
        start = peer(m * piece) - lax.rem(gy, piece)
        slots = hub.at[layer, gx, pl.ds(start, piece)]
        return pltpu.make_async_remote_copy(
            src_ref=slots,
            dst_ref=slots,
            send_sem=col_send.at[layer, k, m],
            recv_sem=col_recv.at[layer, k, m],
            device_id=(lax.rem(gx + k, n_gx), gy),
            device_id_type=MESH,
        )

    def block_copy(layer, k, h):
        rows = pl.ds(h * half, half) if layer else pl.ds(0, tile)
        return pltpu.make_async_remote_copy(
            src_ref=obuf.at[layer, k, rows],
            dst_ref=inc.at[layer, k, rows],
            send_sem=block_send.at[layer, h, k],
            recv_sem=block_recv.at[layer, h, k],
            device_id=(gx, peer(k)),
            device_id_type=MESH,
        )

    def parts(layer):
        return range(HALVES if layer else 1)

    def chunk(s, h):
        return slice(s * part, (s + 1) * part), slice(h * half, (h + 1) * half)

    def hub_onehot():
        row = lax.broadcasted_iota(I32, (16, nodes), 0)
        node = lax.broadcasted_iota(I32, (16, nodes), 1)
        wanted = jnp.full((16, nodes), -1, I32)
        for k in range(hub_dev):
            wanted = jnp.where(row == k, hrows[k], wanted)
        return jnp.where(node == wanted, 1.0, 0.0).astype(BF16)

    def hub_values(ref):
        row = lax.broadcasted_iota(I32, (16, ref.shape[1]), 0)
        rows = jnp.zeros((16, ref.shape[1]), F32)
        for k in range(hub_dev):
            rows = jnp.where(
                row == k, jnp.broadcast_to(ref[pl.ds(hrows[k], 1), :], rows.shape), rows
            )
        return rows

    def rows_of(ref, s, h):
        starts = [b * tile + h * half for b in range(s * part, (s + 1) * part)]
        return jnp.concatenate([ref[i : i + half, :] for i in starts], axis=0)

    def start_rows(layer, picked):
        hub[layer, gx, gy] = picked[0:hub_dev].astype(F32).astype(BF16)
        for k in range(1, n_gy):
            row_copy(layer, k).start()

    def pass_rows_on(layer, m):
        for k in range(max(m * piece, 1), (m + 1) * piece):
            row_copy(layer, k).wait_recv()
        for k in range(1, n_gx):
            col_copy(layer, k, m).start()

    def make_plan():
        count = lcount[0]
        lane = lax.broadcasted_iota(I32, (8, LANES), 1)
        sub = lax.broadcasted_iota(I32, (8, LANES), 0)
        far = jnp.full((8, LANES), LANES * KEY_STEP, I32)
        keys_row, columns = far, []
        for t in range(n_sorted):
            if t < n_local:
                cell = jnp.where(
                    t < count, lcoord[0, t] * blocks + lcoord[1, t], LANES - 1
                )
            else:
                h = t - n_local
                cell = local_cells + hcoord[0, h] * hub_blocks + hcoord[1, h]
            key = cell * KEY_STEP + t
            keys_row = jnp.where(lane == t, key, keys_row)
            if t % 8 == 0:
                columns.append(far)
            columns[-1] = jnp.where(sub == t % 8, key, columns[-1])
        order = jnp.zeros((8, LANES), I32)
        ends = jnp.zeros((8, LANES), I32)
        for i, column in enumerate(columns):
            less = jnp.where(keys_row < column, 1, 0)
            rank = jnp.sum(less, axis=1, keepdims=True)
            order += jnp.where(lane == rank, sub + 8 * i, 0)
            ends += jnp.where(lax.shift_right_logical(column, 6) <= lane, 1, 0)
        plan_vec[0] = jnp.broadcast_to(jnp.sum(order, axis=0, keepdims=True), (8, LANES))
        plan_vec[1] = jnp.broadcast_to(jnp.sum(ends, axis=0, keepdims=True), (8, LANES))

    plan_copy = pltpu.make_async_copy(plan_vec, plan, plan_sem)

    def build_near():
        def body(j, run):
            run = run + tiles[plan[0, 0, j]]
            prefix[j + 1] = run
            return run

        prefix[0] = jnp.zeros((tile, tile), BF16)
        lax.fori_loop(0, n_sorted, body, jnp.zeros((tile, tile), BF16), unroll=8)
        last = jnp.zeros((tile, tile), BF16)
        for cell in range(n_cells):
            now = prefix[plan[1, 0, cell]]
            if cell < local_cells:
                b, c = divmod(cell, blocks)
                near[b, :, c * tile : (c + 1) * tile] = now - last
            else:
                b, c = divmod(cell - local_cells, hub_blocks)
                hubm[b, :, c * tile : (c + 1) * tile] = now - last
            last = now

    def place(dst, u, values, row):
        for b in range(blocks):
            weight = jnp.where(row == b, 1.0, 0.0).astype(BF16)
            dst[b, :, u * tile : (u + 1) * tile] = values * weight

    def place_bound():
        def body(g, carry):
            for u in range(GROUP):
                p = peer(g * GROUP + u)
                place(boundm.at[g], u, btiles[p], brow[p])
            return carry

        lax.fori_loop(0, bound_groups, body, 0)

    def place_hub():
        for u in range(n_hub):
            place(hubm, u, tiles[n_local + u], hcoord[0, u])

    def flat(values):
        return values.reshape(values.shape[0] * values.shape[1], values.shape[2])

    def own_work(src, self_weight):
        own_part[...] = jnp.dot(
            flat(src[...]), self_weight[...], preferred_element_type=F32
        )

    def local_work(src):
        acc[...] = jnp.dot(
            flat(near[...]), flat(src[...]), preferred_element_type=F32
        )

    def wait_blocks(layer, start, stop):
        for k in range(max(start, 1), stop):
            for h in parts(layer):
                block_copy(layer, k, h).wait_recv()

    def bound_sum(layer, g, where, start, stop):
        sources = inc[layer, g * GROUP + start : g * GROUP + stop]
        return jnp.dot(
            flat(boundm[g, where[0], where[1], start * tile : stop * tile]),
            flat(sources),
            preferred_element_type=F32,
        )

    every = (slice(0, blocks), slice(0, tile))

    def early_bound(layer):
        for g in range(bound_groups):
            stop = GROUP if g < bound_groups - 1 else GROUP - 2
            wait_blocks(layer, g * GROUP, g * GROUP + stop)
            acc[...] += bound_sum(layer, g, every, 0, stop)

    def hub_work(layer):
        for m in range(PIECES):
            for k in range(1, n_gx):
                col_copy(layer, k, m).wait_recv()
        hub_all[...] = hub[layer].astype(F32).reshape(hub_all.shape).astype(BF16)
        for u in range(hub_src.shape[0]):
            hub_src[u] = hub_all[u] if dense_hubs else hub_all[hcoord[1, u]]
        acc[...] += jnp.dot(
            flat(hubm[...]), flat(hub_src[...]), preferred_element_type=F32
        )

    def linear(total, inverse, own, neigh_weight):
        neigh = (total * jnp.concatenate([inverse, inverse], axis=1)).astype(BF16)
        return own + jnp.dot(neigh, neigh_weight[...], preferred_element_type=F32)

    def combine(layer, s, h, neigh_weight):
        total = rows_of(acc, s, h) + bound_sum(layer, bound_groups - 1, chunk(s, h), 6, 8)
        return linear(total, rows_of(rdeg, s, h), rows_of(own_part, s, h), neigh_weight)

    def normed(values):
        kept = jnp.maximum(values, 0.0)
        scale = lax.rsqrt(jnp.mean(kept * kept, axis=-1, keepdims=True) + 1e-06)
        return (kept * scale).astype(BF16)

    small[0].wait()
    small[1].wait()
    loads[0].wait()
    picked = jnp.dot(hub_onehot(), flat(feat[...]), preferred_element_type=F32).astype(BF16)
    for k in range(1, n_gy):
        obuf[0, k] = feat[send[peer(k)]]
    pl.semaphore_wait(barrier, n_gy - 1 + gx)
    start_rows(0, picked)
    greet_below()
    for k in range(1, n_gy):
        block_copy(0, k, 0).start()
    for load in loads[1:]:
        load.start()
    for load in small[2:]:
        load.wait()
    make_plan()
    plan_copy.start()
    inc[0, 0] = feat[send[gy]]
    for b in range(blocks):
        inverse = 1.0 / deg[b : b + 1, :].astype(F32)
        rdeg[b * tile : (b + 1) * tile, :] = jnp.broadcast_to(inverse, (tile, tile)).T
    for load in loads[1:]:
        load.wait()
    place_bound()
    hub_bound[...] = jnp.dot(
        hub_onehot(),
        flat(boundm[bound_groups - 1, :, :, 6 * tile : 8 * tile]),
        preferred_element_type=F32,
    ).astype(BF16)
    if not dense_hubs:
        place_hub()
    plan_copy.wait()
    build_near()

    @pl.when(gx + 1 < n_gx)
    def wait_above():
        pl.semaphore_wait(above_in, n_gx - 1 - gx)

    for m in range(PIECES):
        pass_rows_on(0, m)
    own_work(feat, ws1)
    local_work(feat)
    early_bound(0)
    hub_work(0)
    hub_total, hub_inverse, hub_own = hub_values(acc), hub_values(rdeg), hub_values(own_part)
    wait_blocks(0, n_gy - 2, n_gy)
    hub_total += jnp.dot(
        hub_bound[...], flat(inc[0, n_gy - 2 : n_gy]), preferred_element_type=F32
    )
    start_rows(1, normed(linear(hub_total, hub_inverse, hub_own, wn1)))
    for h in range(HALVES):
        for s in range(2):
            values = normed(combine(0, s, h, wn1))
            hidden[chunk(s, h)] = values.reshape(part, half, width)
        rows = slice(h * half, (h + 1) * half)
        for k in range(1, n_gy):
            obuf[1, k, rows] = hidden[send[peer(k)], rows]
            block_copy(1, k, h).start()
    inc[1, 0] = hidden[send[gy]]
    own_work(hidden, ws2)
    for m in range(PIECES):
        pass_rows_on(1, m)
    local_work(hidden)
    early_bound(1)
    hub_work(1)
    wait_blocks(1, n_gy - 2, n_gy)
    for h in range(HALVES):
        for s in range(2):
            out_ref[chunk(s, h)] = combine(1, s, h, wn2).astype(BF16).reshape(part, half, width)

    for layer in range(2):
        for k in range(1, n_gy):
            row_copy(layer, k).wait_send()
            for h in parts(layer):
                block_copy(layer, k, h).wait_send()
        for k in range(1, n_gx):
            for m in range(PIECES):
                col_copy(layer, k, m).wait_send()


def store_kernel(src, dst, store_sem):
    stores = [
        pltpu.make_async_copy(src.at[b], dst.at[b], store_sem.at[b]) for b in range(src.shape[0])
    ]
    for store in stores:
        store.start()
    for store in stores:
        store.wait()


def per_device(
    n_gx,
    n_gy,
    features,
    self_weight_one,
    neigh_weight_one,
    self_weight_two,
    neigh_weight_two,
    degree,
    local_tiles,
    local_coord,
    local_count,
    send_block,
    boundary_tiles,
    boundary_row,
    hub_rows,
    hub_tiles,
    hub_coord,
):
    nodes, width = features.shape
    tile = local_tiles.shape[1]
    blocks = nodes // tile
    hub_dev = hub_rows.shape[0]
    n_local, n_hub = local_tiles.shape[0], hub_tiles.shape[0]
    hub_blocks = n_gx * n_gy * hub_dev // tile
    dense_hubs = blocks * (blocks + hub_blocks) < LANES and n_local + n_hub <= KEY_STEP
    hub_slots = hub_blocks if dense_hubs else n_hub
    vmem = pl.BlockSpec(memory_space=pltpu.VMEM)
    hbm = pl.BlockSpec(memory_space=pltpu.HBM)
    dma = pltpu.SemaphoreType.DMA
    out = pl.pallas_call(
        functools.partial(kernel, n_gx, n_gy, dense_hubs),
        out_shape=pltpu.VMEM((blocks, tile, width), BF16),
        in_specs=[hbm] * 15,
        out_specs=vmem,
        scratch_shapes=[
            pltpu.VMEM((blocks, tile), I32),
            pltpu.SMEM((2, n_local), I32),
            pltpu.SMEM(local_count.shape, I32),
            pltpu.SMEM(send_block.shape, I32),
            pltpu.SMEM(boundary_row.shape, I32),
            pltpu.SMEM(hub_rows.shape, I32),
            pltpu.SMEM((2, n_hub), I32),
            pltpu.VMEM((blocks, tile, width), BF16),
            pltpu.VMEM((width, width), BF16),
            pltpu.VMEM((width, width), BF16),
            pltpu.VMEM((width, width), BF16),
            pltpu.VMEM((width, width), BF16),
            pltpu.VMEM((n_local + n_hub, tile, tile), BF16),
            pltpu.VMEM(boundary_tiles.shape, BF16),
            pltpu.VMEM((2, 8, LANES), I32),
            pltpu.SMEM((2, 8, LANES), I32),
            pltpu.VMEM((n_local + n_hub + 1, tile, tile), BF16),
            pltpu.VMEM((blocks, tile, nodes), BF16),
            pltpu.VMEM((blocks, tile, hub_slots * tile), BF16),
            pltpu.VMEM((n_gy // GROUP, blocks, tile, GROUP * tile), BF16),
            pltpu.VMEM((hub_slots, tile, width), BF16),
            pltpu.VMEM((2, n_gy, tile, width), BF16),
            pltpu.VMEM((2, n_gy, tile, width), BF16),
            pltpu.VMEM((2, n_gx, n_gy, hub_dev, width), BF16),
            pltpu.VMEM((hub_blocks, tile, width), BF16),
            pltpu.VMEM((blocks, tile, width), BF16),
            pltpu.VMEM((nodes, width), F32),
            pltpu.VMEM((nodes, width), F32),
            pltpu.VMEM((nodes, tile), F32),
            pltpu.VMEM((16, 2 * tile), BF16),
            dma((15,)),
            dma,
            pltpu.SemaphoreType.REGULAR,
            dma((2, HALVES, n_gy)),
            dma((2, HALVES, n_gy)),
            dma((2, n_gy)),
            dma((2, n_gy)),
            dma((2, n_gx, PIECES)),
            dma((2, n_gx, PIECES)),
        ],
        compiler_params=pltpu.CompilerParams(
            collective_id=0, has_side_effects=True, vmem_limit_bytes=56 * 2**20
        ),
        name="sage_two_layers",
    )(
        degree.reshape(blocks, tile),
        local_coord.T,
        local_count,
        send_block,
        boundary_row,
        hub_rows,
        hub_coord.T,
        features.reshape(blocks, tile, width),
        self_weight_one,
        neigh_weight_one,
        self_weight_two,
        neigh_weight_two,
        local_tiles,
        boundary_tiles,
        hub_tiles,
    )
    out = pl.pallas_call(
        store_kernel,
        out_shape=jax.ShapeDtypeStruct((blocks, tile, width), BF16),
        in_specs=[vmem],
        out_specs=hbm,
        scratch_shapes=[dma((blocks,))],
        name="store_result",
    )(pltpu.with_memory_space_constraint(out, pltpu.VMEM))
    return out.reshape(nodes, width)


def solution(mesh):
    placed = (
        P(("gx", "gy"), None),
        P(),
        P(),
        P(),
        P(),
        P(("gx", "gy")),
        P(("gx", "gy"), None, None),
        P(("gx", "gy"), None),
        P(("gx", "gy")),
        P(("gx", "gy")),
        P(("gx", "gy"), None, None),
        P(("gx", "gy")),
        P(("gx", "gy")),
        P(("gx", "gy"), None, None),
        P(("gx", "gy"), None),
    )
    return jax.shard_map(
        functools.partial(per_device, mesh.shape["gx"], mesh.shape["gy"]),
        mesh=mesh,
        in_specs=placed,
        out_specs=P(("gx", "gy"), None),
        check_vma=False,
    )
```

```python
import functools

import jax
import jax.numpy as jnp
from jax import lax
from jax.experimental import pallas as pl
from jax.experimental.pallas import tpu as pltpu
from jax.sharding import PartitionSpec as P

MESH = pl.DeviceIdType.MESH
GROUP = 8
LANES = 128
KEY_STEP = 64
PIECES = 2
HALVES = 1
F32 = jnp.float32
BF16 = jnp.bfloat16
I32 = jnp.int32


def kernel(
    n_gx,
    n_gy,
    dense_hubs,
    deg_any,
    lcoord_any,
    lcount_any,
    send_any,
    brow_any,
    hrows_any,
    hcoord_any,
    feat_any,
    ws1_any,
    wn1_any,
    ws2_any,
    wn2_any,
    ltiles_any,
    btiles_any,
    htiles_any,
    out_ref,
    deg,
    lcoord,
    lcount,
    send,
    brow,
    hrows,
    hcoord,
    feat,
    ws1,
    wn1,
    ws2,
    wn2,
    tiles,
    btiles,
    plan_vec,
    plan,
    prefix,
    near,
    hubm,
    boundm,
    hub_src,
    obuf,
    inc,
    hub,
    hub_all,
    hidden,
    acc,
    own_part,
    rdeg,
    hub_bound,
    load_sem,
    plan_sem,
    above_in,
    block_send,
    block_recv,
    row_send,
    row_recv,
    col_send,
    col_recv,
):
    gx = lax.axis_index("gx")
    gy = lax.axis_index("gy")
    blocks, tile, width = feat.shape
    nodes = blocks * tile
    n_local = ltiles_any.shape[0]
    n_hub = htiles_any.shape[0]
    hub_blocks = hub_all.shape[0]
    bound_groups = n_gy // GROUP
    hub_dev = hrows.shape[0]
    piece = n_gy // PIECES
    part = blocks // 2
    half = tile // HALVES
    local_cells = blocks * blocks
    n_cells = local_cells + (blocks * hub_blocks if dense_hubs else 0)
    n_sorted = n_local + (n_hub if dense_hubs else 0)

    def peer(k):
        place, other = 1, 0
        while place < n_gy:
            other += lax.rem(lax.div(gy, place) + lax.div(k, place), 2) * place
            place *= 2
        return other

    barrier = pltpu.get_barrier_semaphore()
    for k in reversed(range(1, n_gy)):
        pl.semaphore_signal(
            barrier, inc=1, device_id=(gx, peer(k)), device_id_type=MESH
        )
    for k in range(1, n_gx):

        @pl.when(gx + k < n_gx)
        def greet_above():
            pl.semaphore_signal(
                barrier, inc=1, device_id=(gx + k, gy), device_id_type=MESH
            )

    def greet_below():
        for k in range(1, n_gx):

            @pl.when(gx >= k)
            def greet():
                pl.semaphore_signal(
                    above_in, inc=1, device_id=(gx - k, gy), device_id_type=MESH
                )

    loads = [
        pltpu.make_async_copy(src, dst, load_sem.at[i])
        for i, (src, dst) in enumerate(
            (
                (feat_any, feat),
                (ltiles_any, tiles.at[0:n_local]),
                (btiles_any, btiles),
                (htiles_any, tiles.at[n_local : n_local + n_hub]),
                (ws1_any, ws1),
                (wn1_any, wn1),
                (ws2_any, ws2),
                (wn2_any, wn2),
            )
        )
    ]
    small = [
        pltpu.make_async_copy(src, dst, load_sem.at[len(loads) + i])
        for i, (src, dst) in enumerate(
            (
                (send_any, send),
                (hrows_any, hrows),
                (deg_any, deg),
                (lcoord_any, lcoord),
                (lcount_any, lcount),
                (brow_any, brow),
                (hcoord_any, hcoord),
            )
        )
    ]
    loads[0].start()
    for load in small:
        load.start()

    def row_copy(layer, k):
        slot = hub.at[layer, gx, gy]
        return pltpu.make_async_remote_copy(
            src_ref=slot,
            dst_ref=slot,
            send_sem=row_send.at[layer, k],
            recv_sem=row_recv.at[layer, k],
            device_id=(gx, peer(k)),
            device_id_type=MESH,
        )

    def col_copy(layer, k, m):
        start = peer(m * piece) - lax.rem(gy, piece)
        slots = hub.at[layer, gx, pl.ds(start, piece)]
        return pltpu.make_async_remote_copy(
            src_ref=slots,
            dst_ref=slots,
            send_sem=col_send.at[layer, k, m],
            recv_sem=col_recv.at[layer, k, m],
            device_id=(lax.rem(gx + k, n_gx), gy),
            device_id_type=MESH,
        )

    def block_copy(layer, k, h):
        rows = pl.ds(h * half, half) if layer else pl.ds(0, tile)
        return pltpu.make_async_remote_copy(
            src_ref=obuf.at[layer, k, rows],
            dst_ref=inc.at[layer, k, rows],
            send_sem=block_send.at[layer, h, k],
            recv_sem=block_recv.at[layer, h, k],
            device_id=(gx, peer(k)),
            device_id_type=MESH,
        )

    def parts(layer):
        return range(HALVES if layer else 1)

    def chunk(s, h):
        return slice(s * part, (s + 1) * part), slice(h * half, (h + 1) * half)

    def hub_onehot():
        row = lax.broadcasted_iota(I32, (16, nodes), 0)
        node = lax.broadcasted_iota(I32, (16, nodes), 1)
        wanted = jnp.full((16, nodes), -1, I32)
        for k in range(hub_dev):
            wanted = jnp.where(row == k, hrows[k], wanted)
        return jnp.where(node == wanted, 1.0, 0.0).astype(BF16)

    def hub_values(ref):
        row = lax.broadcasted_iota(I32, (16, ref.shape[1]), 0)
        rows = jnp.zeros((16, ref.shape[1]), F32)
        for k in range(hub_dev):
            rows = jnp.where(
                row == k, jnp.broadcast_to(ref[pl.ds(hrows[k], 1), :], rows.shape), rows
            )
        return rows

    def rows_of(ref, s, h):
        starts = [b * tile + h * half for b in range(s * part, (s + 1) * part)]
        return jnp.concatenate([ref[i : i + half, :] for i in starts], axis=0)

    def start_rows(layer, picked):
        hub[layer, gx, gy] = picked[0:hub_dev].astype(F32).astype(BF16)
        for k in range(1, n_gy):
            row_copy(layer, k).start()

    def pass_rows_on(layer, m):
        for k in range(max(m * piece, 1), (m + 1) * piece):
            row_copy(layer, k).wait_recv()
        for i in range(n_gx - 1):
            to = i + jnp.where(gx <= i, 1, 0)
            col_copy(layer, lax.rem(to - gx + n_gx, n_gx), m).start()

    def make_plan():
        count = lcount[0]
        lane = lax.broadcasted_iota(I32, (8, LANES), 1)
        sub = lax.broadcasted_iota(I32, (8, LANES), 0)
        far = jnp.full((8, LANES), LANES * KEY_STEP, I32)
        keys_row, columns = far, []
        for t in range(n_sorted):
            if t < n_local:
                cell = jnp.where(
                    t < count, lcoord[0, t] * blocks + lcoord[1, t], LANES - 1
                )
            else:
                h = t - n_local
                cell = local_cells + hcoord[0, h] * hub_blocks + hcoord[1, h]
            key = cell * KEY_STEP + t
            keys_row = jnp.where(lane == t, key, keys_row)
            if t % 8 == 0:
                columns.append(far)
            columns[-1] = jnp.where(sub == t % 8, key, columns[-1])
        order = jnp.zeros((8, LANES), I32)
        ends = jnp.zeros((8, LANES), I32)
        for i, column in enumerate(columns):
            less = jnp.where(keys_row < column, 1, 0)
            rank = jnp.sum(less, axis=1, keepdims=True)
            order += jnp.where(lane == rank, sub + 8 * i, 0)
            ends += jnp.where(lax.shift_right_logical(column, 6) <= lane, 1, 0)
        plan_vec[0] = jnp.broadcast_to(jnp.sum(order, axis=0, keepdims=True), (8, LANES))
        plan_vec[1] = jnp.broadcast_to(jnp.sum(ends, axis=0, keepdims=True), (8, LANES))

    plan_copy = pltpu.make_async_copy(plan_vec, plan, plan_sem)

    def build_near():
        def body(j, run):
            run = run + tiles[plan[0, 0, j]]
            prefix[j + 1] = run
            return run

        prefix[0] = jnp.zeros((tile, tile), BF16)
        lax.fori_loop(0, n_sorted, body, jnp.zeros((tile, tile), BF16), unroll=8)
        last = jnp.zeros((tile, tile), BF16)
        for cell in range(n_cells):
            now = prefix[plan[1, 0, cell]]
            if cell < local_cells:
                b, c = divmod(cell, blocks)
                near[b, :, c * tile : (c + 1) * tile] = now - last
            else:
                b, c = divmod(cell - local_cells, hub_blocks)
                hubm[b, :, c * tile : (c + 1) * tile] = now - last
            last = now

    def place(dst, u, values, row):
        for b in range(blocks):
            weight = jnp.where(row == b, 1.0, 0.0).astype(BF16)
            dst[b, :, u * tile : (u + 1) * tile] = values * weight

    def place_bound():
        def body(g, carry):
            for u in range(GROUP):
                p = peer(g * GROUP + u)
                place(boundm.at[g], u, btiles[p], brow[p])
            return carry

        lax.fori_loop(0, bound_groups, body, 0)

    def place_hub():
        for u in range(n_hub):
            place(hubm, u, tiles[n_local + u], hcoord[0, u])

    def flat(values):
        return values.reshape(values.shape[0] * values.shape[1], values.shape[2])

    def own_work(src, self_weight):
        own_part[...] = jnp.dot(
            flat(src[...]), self_weight[...], preferred_element_type=F32
        )

    def local_work(src):
        acc[...] = jnp.dot(
            flat(near[...]), flat(src[...]), preferred_element_type=F32
        )

    def wait_blocks(layer, start, stop):
        for k in range(max(start, 1), stop):
            for h in parts(layer):
                block_copy(layer, k, h).wait_recv()

    def bound_sum(layer, g, where, start, stop):
        sources = inc[layer, g * GROUP + start : g * GROUP + stop]
        return jnp.dot(
            flat(boundm[g, where[0], where[1], start * tile : stop * tile]),
            flat(sources),
            preferred_element_type=F32,
        )

    every = (slice(0, blocks), slice(0, tile))

    def early_bound(layer):
        for g in range(bound_groups):
            stop = GROUP if g < bound_groups - 1 else GROUP - 2
            wait_blocks(layer, g * GROUP, g * GROUP + stop)
            acc[...] += bound_sum(layer, g, every, 0, stop)

    def hub_work(layer):
        for m in range(PIECES):
            for k in range(1, n_gx):
                col_copy(layer, k, m).wait_recv()
        hub_all[...] = hub[layer].astype(F32).reshape(hub_all.shape).astype(BF16)
        for u in range(hub_src.shape[0]):
            hub_src[u] = hub_all[u] if dense_hubs else hub_all[hcoord[1, u]]
        acc[...] += jnp.dot(
            flat(hubm[...]), flat(hub_src[...]), preferred_element_type=F32
        )

    def linear(total, inverse, own, neigh_weight):
        neigh = (total * jnp.concatenate([inverse, inverse], axis=1)).astype(BF16)
        return own + jnp.dot(neigh, neigh_weight[...], preferred_element_type=F32)

    def combine(layer, s, h, neigh_weight):
        total = rows_of(acc, s, h) + bound_sum(layer, bound_groups - 1, chunk(s, h), 6, 8)
        return linear(total, rows_of(rdeg, s, h), rows_of(own_part, s, h), neigh_weight)

    def normed(values):
        kept = jnp.maximum(values, 0.0)
        scale = lax.rsqrt(jnp.mean(kept * kept, axis=-1, keepdims=True) + 1e-06)
        return (kept * scale).astype(BF16)

    small[0].wait()
    small[1].wait()
    loads[0].wait()
    picked = jnp.dot(hub_onehot(), flat(feat[...]), preferred_element_type=F32).astype(BF16)
    for k in range(1, n_gy):
        obuf[0, k] = feat[send[peer(k)]]
    pl.semaphore_wait(barrier, n_gy - 1 + gx)
    start_rows(0, picked)
    greet_below()
    for k in range(1, n_gy):
        block_copy(0, k, 0).start()
    for load in loads[1:]:
        load.start()
    for load in small[2:]:
        load.wait()
    make_plan()
    plan_copy.start()
    inc[0, 0] = feat[send[gy]]
    for b in range(blocks):
        inverse = 1.0 / deg[b : b + 1, :].astype(F32)
        rdeg[b * tile : (b + 1) * tile, :] = jnp.broadcast_to(inverse, (tile, tile)).T
    for load in loads[1:]:
        load.wait()
    place_bound()
    hub_bound[...] = jnp.dot(
        hub_onehot(),
        flat(boundm[bound_groups - 1, :, :, 6 * tile : 8 * tile]),
        preferred_element_type=F32,
    ).astype(BF16)
    if not dense_hubs:
        place_hub()
    plan_copy.wait()
    build_near()

    @pl.when(gx + 1 < n_gx)
    def wait_above():
        pl.semaphore_wait(above_in, n_gx - 1 - gx)

    for m in range(PIECES):
        pass_rows_on(0, m)
    own_work(feat, ws1)
    local_work(feat)
    early_bound(0)
    hub_work(0)
    hub_total, hub_inverse, hub_own = hub_values(acc), hub_values(rdeg), hub_values(own_part)
    wait_blocks(0, n_gy - 2, n_gy)
    hub_total += jnp.dot(
        hub_bound[...], flat(inc[0, n_gy - 2 : n_gy]), preferred_element_type=F32
    )
    start_rows(1, normed(linear(hub_total, hub_inverse, hub_own, wn1)))
    for h in range(HALVES):
        for s in range(2):
            values = normed(combine(0, s, h, wn1))
            hidden[chunk(s, h)] = values.reshape(part, half, width)
        rows = slice(h * half, (h + 1) * half)
        for k in range(1, n_gy):
            obuf[1, k, rows] = hidden[send[peer(k)], rows]
            block_copy(1, k, h).start()
    inc[1, 0] = hidden[send[gy]]
    own_work(hidden, ws2)
    for m in range(PIECES):
        pass_rows_on(1, m)
    local_work(hidden)
    early_bound(1)
    hub_work(1)
    wait_blocks(1, n_gy - 2, n_gy)
    for h in range(HALVES):
        for s in range(2):
            out_ref[chunk(s, h)] = combine(1, s, h, wn2).astype(BF16).reshape(part, half, width)

    for layer in range(2):
        for k in range(1, n_gy):
            row_copy(layer, k).wait_send()
            for h in parts(layer):
                block_copy(layer, k, h).wait_send()
        for k in range(1, n_gx):
            for m in range(PIECES):
                col_copy(layer, k, m).wait_send()


def store_kernel(src, dst, store_sem):
    stores = [
        pltpu.make_async_copy(src.at[b], dst.at[b], store_sem.at[b]) for b in range(src.shape[0])
    ]
    for store in stores:
        store.start()
    for store in stores:
        store.wait()


def per_device(
    n_gx,
    n_gy,
    features,
    self_weight_one,
    neigh_weight_one,
    self_weight_two,
    neigh_weight_two,
    degree,
    local_tiles,
    local_coord,
    local_count,
    send_block,
    boundary_tiles,
    boundary_row,
    hub_rows,
    hub_tiles,
    hub_coord,
):
    nodes, width = features.shape
    tile = local_tiles.shape[1]
    blocks = nodes // tile
    hub_dev = hub_rows.shape[0]
    n_local, n_hub = local_tiles.shape[0], hub_tiles.shape[0]
    hub_blocks = n_gx * n_gy * hub_dev // tile
    dense_hubs = blocks * (blocks + hub_blocks) < LANES and n_local + n_hub <= KEY_STEP
    hub_slots = hub_blocks if dense_hubs else n_hub
    vmem = pl.BlockSpec(memory_space=pltpu.VMEM)
    hbm = pl.BlockSpec(memory_space=pltpu.HBM)
    dma = pltpu.SemaphoreType.DMA
    out = pl.pallas_call(
        functools.partial(kernel, n_gx, n_gy, dense_hubs),
        out_shape=pltpu.VMEM((blocks, tile, width), BF16),
        in_specs=[hbm] * 15,
        out_specs=vmem,
        scratch_shapes=[
            pltpu.VMEM((blocks, tile), I32),
            pltpu.SMEM((2, n_local), I32),
            pltpu.SMEM(local_count.shape, I32),
            pltpu.SMEM(send_block.shape, I32),
            pltpu.SMEM(boundary_row.shape, I32),
            pltpu.SMEM(hub_rows.shape, I32),
            pltpu.SMEM((2, n_hub), I32),
            pltpu.VMEM((blocks, tile, width), BF16),
            pltpu.VMEM((width, width), BF16),
            pltpu.VMEM((width, width), BF16),
            pltpu.VMEM((width, width), BF16),
            pltpu.VMEM((width, width), BF16),
            pltpu.VMEM((n_local + n_hub, tile, tile), BF16),
            pltpu.VMEM(boundary_tiles.shape, BF16),
            pltpu.VMEM((2, 8, LANES), I32),
            pltpu.SMEM((2, 8, LANES), I32),
            pltpu.VMEM((n_local + n_hub + 1, tile, tile), BF16),
            pltpu.VMEM((blocks, tile, nodes), BF16),
            pltpu.VMEM((blocks, tile, hub_slots * tile), BF16),
            pltpu.VMEM((n_gy // GROUP, blocks, tile, GROUP * tile), BF16),
            pltpu.VMEM((hub_slots, tile, width), BF16),
            pltpu.VMEM((2, n_gy, tile, width), BF16),
            pltpu.VMEM((2, n_gy, tile, width), BF16),
            pltpu.VMEM((2, n_gx, n_gy, hub_dev, width), BF16),
            pltpu.VMEM((hub_blocks, tile, width), BF16),
            pltpu.VMEM((blocks, tile, width), BF16),
            pltpu.VMEM((nodes, width), F32),
            pltpu.VMEM((nodes, width), F32),
            pltpu.VMEM((nodes, tile), F32),
            pltpu.VMEM((16, 2 * tile), BF16),
            dma((15,)),
            dma,
            pltpu.SemaphoreType.REGULAR,
            dma((2, HALVES, n_gy)),
            dma((2, HALVES, n_gy)),
            dma((2, n_gy)),
            dma((2, n_gy)),
            dma((2, n_gx, PIECES)),
            dma((2, n_gx, PIECES)),
        ],
        compiler_params=pltpu.CompilerParams(
            collective_id=0, has_side_effects=True, vmem_limit_bytes=56 * 2**20
        ),
        name="sage_two_layers",
    )(
        degree.reshape(blocks, tile),
        local_coord.T,
        local_count,
        send_block,
        boundary_row,
        hub_rows,
        hub_coord.T,
        features.reshape(blocks, tile, width),
        self_weight_one,
        neigh_weight_one,
        self_weight_two,
        neigh_weight_two,
        local_tiles,
        boundary_tiles,
        hub_tiles,
    )
    out = pl.pallas_call(
        store_kernel,
        out_shape=jax.ShapeDtypeStruct((blocks, tile, width), BF16),
        in_specs=[vmem],
        out_specs=hbm,
        scratch_shapes=[dma((blocks,))],
        name="store_result",
    )(pltpu.with_memory_space_constraint(out, pltpu.VMEM))
    return out.reshape(nodes, width)


def solution(mesh):
    placed = (
        P(("gx", "gy"), None),
        P(),
        P(),
        P(),
        P(),
        P(("gx", "gy")),
        P(("gx", "gy"), None, None),
        P(("gx", "gy"), None),
        P(("gx", "gy")),
        P(("gx", "gy")),
        P(("gx", "gy"), None, None),
        P(("gx", "gy")),
        P(("gx", "gy")),
        P(("gx", "gy"), None, None),
        P(("gx", "gy"), None),
    )
    return jax.shard_map(
        functools.partial(per_device, mesh.shape["gx"], mesh.shape["gy"]),
        mesh=mesh,
        in_specs=placed,
        out_specs=P(("gx", "gy"), None),
        check_vma=False,
    )
```
